32 devices in a mesh: elem: 16 (over z, x, core), band: 2 (over y).
Axes of the slice: x: 2, y: 2, z: 4, core: 2. Of those that a mesh axis runs over, the one named last changes fastest.
Arguments:
- basis: bfloat16 [256, 32, 16, 160], P('band', 'elem'), may hold values from -8 to 8
- hamiltonian: bfloat16 [32, 16, 7, 160, 160], P('elem'), may hold values from -0.09375 to 0.09375
- neighbours: int32 [32, 16, 6], P('elem'), may hold values from 0 to 511, as said below
Outputs:
- filtered: bfloat16 [256, 32, 16, 160], P('band', 'elem')
- intersection: float32 [256, 256], P('elem', 'band')
- projected: float32 [256, 256], P('elem', 'band')
The draws below stay inside these ranges and needn't reach their ends.
Inputs may be any that keep to these rules, and one draw needn't show every extreme that they name: neighbours[z, s, d] = z2 * 16 + s2 names the element (z2, s2) that shares face d with element (z, s) on a periodic grid of 4 x 4 x 32 cells, whose cells are stored within each layer in an order of the draw; faces 0 to 3 lie in the same layer z, face 4 in layer z - 1 and face 5 in layer z + 1, both modulo 32.
All inputs are finite; a program needn't handle non-finite values.
Results may differ from the reference program's by a relative error of at most 0.0075.
Values may be sent and summed in bfloat16 or wider, within the bound.
A program may use at most 64 MiB of HBM per device.

```python
import jax
import jax.numpy as jnp

NB = 160
BANDS = 256
CX = 4
CY = 4
DEGREE = 4
CXY = 16
NZ = 32


def draw_neighbours(key, part):
    layer_keys = jax.random.split(jax.random.fold_in(key, 17), NZ)
    cells = CX * CY
    orders = jax.vmap(lambda k: jax.random.permutation(k, cells))(layer_keys).astype(jnp.int32)
    places = jnp.argsort(orders, axis=1).astype(jnp.int32)
    across = orders // CY
    along = orders % CY
    minus_x = (across - 1) % CX * CY + along
    plus_x = (across + 1) % CX * CY + along
    minus_y = across * CY + (along - 1) % CY
    plus_y = across * CY + (along + 1) % CY
    layers = jnp.arange(NZ).astype(jnp.int32)[:, None] * jnp.ones((1, cells), jnp.int32)
    same = [jnp.take_along_axis(places, target, axis=1) + layers * cells for target in (minus_x, plus_x, minus_y, plus_y)]
    below = jnp.roll(places, 1, axis=0)
    above = jnp.roll(places, -1, axis=0)
    lower = jnp.take_along_axis(below, orders, axis=1) + (layers - 1) % NZ * cells
    upper = jnp.take_along_axis(above, orders, axis=1) + (layers + 1) % NZ * cells
    return jnp.stack(same + [lower, upper], axis=-1).astype(jnp.int32)


def draw_basis(key, part):
    base = jax.random.fold_in(key, 29)
    key_noise, key_common, key_group, key_weight = jax.random.split(base, 4)
    families = 16
    shape = (BANDS, NZ, CX * CY, NB)
    groups = jax.random.randint(key_group, (BANDS,), 0, families).astype(jnp.int32)
    noise = jax.random.normal(key_noise, shape, jnp.float32)
    common = jax.random.normal(key_common, (families, NZ, CX * CY, NB), jnp.float32)
    weight = jax.random.normal(key_weight, (BANDS, 1, 1, 1), jnp.float32)
    shared = jnp.take(common, groups, axis=0)
    value = noise + weight * shared
    return jnp.clip(value, -8.0, 8.0).astype(jnp.bfloat16)


def block_levels(stream_key, extent, cuts, low, largest):
    def one(dim, shards_of):
        heights = jax.random.uniform(jax.random.fold_in(jax.random.fold_in(stream_key, 6), dim), (shards_of,), jnp.float32, low / len(cuts), largest / len(cuts))
        return jnp.repeat(jnp.exp(heights), extent[dim] // shards_of).reshape((-1,) + (1,) * (len(extent) - dim - 1))

    level = one(*cuts[0])
    for cut in cuts[1:]:
        level = level * one(*cut)
    return level


def centred(rng, shape, spread, reach, shards=(), dtype=jnp.bfloat16):
    loudness = block_levels(rng, shape, shards, -0.22, 0.18) if shards else 1.0
    array = jax.random.normal(rng, shape, jnp.float32) * spread * loudness
    return jnp.minimum(jnp.maximum(array, -reach), reach).astype(dtype)


def setup_inputs(seed: int = 0) -> dict:
    seeds = jax.random.split(jax.random.key(seed), 4)
    basis = draw_basis(jax.random.fold_in(seeds[3], 71), 0)
    hamiltonian = centred(seeds[1], (NZ, CXY, 7, NB, NB), (28 * NB) ** -0.5, 0.09375, ((0, 16),))
    neighbours = draw_neighbours(jax.random.fold_in(seeds[3], 71), 0)
    return dict(basis=basis, hamiltonian=hamiltonian, neighbours=neighbours)


def apply_blocks(flat, blocks, table):
    total = jnp.zeros(flat.shape, jnp.float32)
    for face in range(7):
        picked = jnp.take(flat, table[:, face], axis=1).astype(jnp.float32)
        total = total + jnp.einsum("eij,bej->bei", blocks[:, face].astype(jnp.float32), picked)
    return total


def reference(basis, hamiltonian, neighbours):
    count = NZ * CX * CY
    flat = basis.reshape(BANDS, count, NB)
    blocks = hamiltonian.reshape(count, 7, NB, NB)
    own = jnp.arange(count).astype(jnp.int32)[:, None]
    table = jnp.concatenate([own, neighbours.reshape(count, 6).astype(jnp.int32)], axis=1)
    previous = flat
    current = apply_blocks(flat, blocks, table).astype(jnp.bfloat16)
    for step in range(DEGREE - 1):
        following = (2.0 * apply_blocks(current, blocks, table) - previous.astype(jnp.float32)).astype(jnp.bfloat16)
        previous, current = current, following
    image = apply_blocks(current, blocks, table).astype(jnp.bfloat16)
    factor = 1.0 / (count * NB)
    left = current.astype(jnp.float32)
    intersection = jnp.einsum("aei,bei->ab", left, left) * factor
    projected = jnp.einsum("aei,bei->ab", left, image.astype(jnp.float32)) * factor
    return current.reshape(BANDS, NZ, CX * CY, NB), intersection, projected
```

```python
import functools

import jax
import jax.numpy as jnp
from jax import lax
from jax.experimental import pallas as pl
from jax.experimental.pallas import tpu as pltpu
from jax.sharding import PartitionSpec as P

DEGREE = 4
MESH = pl.DeviceIdType.MESH
F32 = jnp.float32
BF16 = jnp.bfloat16


def dot(a, b):
    return jnp.dot(a, b, preferred_element_type=F32)


def kernel(
    geom,
    tab,
    y0,
    ham_hbm,
    ft,
    s_out,
    p_out,
    ham,
    buf_a,
    buf_b,
    lo0,
    lo1,
    hi0,
    hi1,
    acc,
    it,
    others,
    parts,
    got1,
    mid,
    got2,
    ham_sem,
    send_sem,
    recv_sem,
    fsend,
    frecv,
    r1send,
    r1recv,
    r2send,
    r2recv,
):
    n, nband, cells, n1, n2, rows, factor = geom
    total = 2 * cells
    funcs, bands = y0.shape[1], y0.shape[2]
    me = lax.axis_index("elem")
    bme = lax.axis_index("band")
    right, left = lax.rem(me + 1, n), lax.rem(me + n - 1, n)
    group, member = me // n1, me % n1

    hcopies = []
    hparts = ham_sem.shape[0]
    for c in range(hparts):
        size = ham.shape[0] // hparts
        window = pl.ds(c * size, size)
        hc = pltpu.make_async_copy(ham_hbm.at[window], ham.at[window], ham_sem.at[c])
        hc.start()
        hcopies.append(hc)

    barrier = pltpu.get_barrier_semaphore()
    peers = [{"elem": left}, {"elem": right}]
    for j in range(1, nband):
        peers.append({"band": lax.rem(bme + j, nband)})
    for j in range(1, n1):
        peers.append({"elem": group * n1 + lax.rem(member + j, n1)})
    for j in range(1, n2):
        peers.append({"elem": lax.rem(group + j, n2) * n1 + member})
    for peer in peers:
        pl.semaphore_signal(barrier, inc=1, device_id=peer, device_id_type=MESH)
    pl.semaphore_wait(barrier, len(peers))

    los, his = (lo0, lo1), (hi0, hi1)

    def send_up(step, source):
        copy = pltpu.make_async_remote_copy(
            src_ref=source.at[pl.ds(cells, cells)],
            dst_ref=los[step % 2],
            send_sem=send_sem.at[step, 0],
            recv_sem=recv_sem.at[step, 0],
            device_id={"elem": right},
            device_id_type=MESH,
        )
        copy.start()
        return copy

    def send_down(step, source):
        copy = pltpu.make_async_remote_copy(
            src_ref=source.at[pl.ds(0, cells)],
            dst_ref=his[step % 2],
            send_sem=send_sem.at[step, 1],
            recv_sem=recv_sem.at[step, 1],
            device_id={"elem": left},
            device_id_type=MESH,
        )
        copy.start()
        return copy

    fcopies = []

    def send_field(layer):
        window = pl.ds(layer * cells, cells)
        for j in range(1, nband):
            copy = pltpu.make_async_remote_copy(
                src_ref=buf_a.at[window],
                dst_ref=others.at[j - 1, window],
                send_sem=fsend.at[j - 1, layer],
                recv_sem=frecv.at[j - 1, layer],
                device_id={"band": lax.rem(bme + j, nband)},
                device_id_type=MESH,
            )
            copy.start()
            fcopies.append((j, layer, copy))

    up, down = send_up(0, y0), send_down(0, y0)
    for hc in hcopies:
        hc.wait()

    current = y0
    for step in range(DEGREE + 1):
        last = step == DEGREE
        target = buf_b if step % 2 == 0 else buf_a
        prior = y0 if step == 1 else target

        def local(e, carry, current=current):
            six = e // cells
            base = e * 7
            total_ = dot(ham[base], current[e])
            for d in range(4):
                total_ += dot(ham[base + d + 1], current[tab[e * 6 + d]])
            total_ += dot(ham[base + 6 - six], current[tab[e * 6 + 4]])
            acc[e] = total_
            return carry

        lax.fori_loop(0, total, local, 0)

        def finish(e, carry, step=step, halo=None, face=0, target=target, prior=prior):
            value = acc[e] + dot(ham[e * 7 + face], halo[tab[e * 6 + 5]])
            if step > 0 and step < DEGREE:
                value = 2.0 * value - prior[e].astype(F32)
            if step < DEGREE:
                target[e] = value.astype(BF16)
            if step == DEGREE:
                it[e] = value.T.astype(BF16)
            return carry

        up_next = down_next = None
        down.wait_recv()
        lax.fori_loop(
            cells, total, functools.partial(finish, halo=his[step % 2], face=6), 0
        )
        if not last:
            up_next = send_up(step + 1, target)
        if step == DEGREE - 1:
            send_field(1)
        up.wait_recv()
        lax.fori_loop(
            0, cells, functools.partial(finish, halo=los[step % 2], face=5), 0
        )
        if not last:
            down_next = send_down(step + 1, target)
        if step == DEGREE - 1:
            send_field(0)

            def turn(e, carry):
                ft[e] = buf_a[e].astype(F32).T.astype(BF16)
                return carry

            lax.fori_loop(0, total, turn, 0)
        up.wait_send()
        down.wait_send()
        up, down = up_next, down_next
        current = target

    per = bands // rows

    def gram(field, first, count, state):
        def body(e, carry):
            s, p = carry
            v = field(e)
            return s + dot(ft[e], v), p + dot(it[e], v)

        return lax.fori_loop(first, first + count, body, state)

    def put(who, state):
        for t in range(2):
            block = state[t].T.reshape(per, rows, bands)
            for i in range(per):
                r = who * per + i
                parts[r % n1, r // n1, t] = block[i]

    zero = jnp.zeros((bands, bands), F32)
    put(bme, gram(lambda e: buf_a[e], 0, total, (zero, zero)))
    for j in range(1, nband):
        state = (zero, zero)
        for jj, layer, copy in fcopies:
            if jj == j:
                copy.wait_recv()
                state = gram(lambda e: others[j - 1, e], layer * cells, cells, state)
        put(lax.rem(bme + nband - j, nband), state)

    copies = []
    for j in range(1, n1):
        to = lax.rem(member + j, n1)
        copy = pltpu.make_async_remote_copy(
            src_ref=parts.at[to],
            dst_ref=got1.at[j - 1],
            send_sem=r1send.at[j - 1],
            recv_sem=r1recv.at[j - 1],
            device_id={"elem": group * n1 + to},
            device_id_type=MESH,
        )
        copy.start()
        copies.append(copy)
    for _, _, copy in fcopies:
        copy.wait_send()
    running = parts[member]
    for j, copy in enumerate(copies):
        copy.wait_recv()
        running += got1[j]
    mid[...] = running
    copies2 = []
    for j in range(1, n2):
        to = lax.rem(group + j, n2)
        copy = pltpu.make_async_remote_copy(
            src_ref=mid.at[to],
            dst_ref=got2.at[j - 1],
            send_sem=r2send.at[j - 1],
            recv_sem=r2recv.at[j - 1],
            device_id={"elem": to * n1 + member},
            device_id_type=MESH,
        )
        copy.start()
        copies2.append(copy)
    for copy in copies:
        copy.wait_send()
    final = mid[group]
    for j, copy in enumerate(copies2):
        copy.wait_recv()
        final += got2[j]
    for copy in copies2:
        copy.wait_send()
    s_out[...] = final[0] * factor
    p_out[...] = final[1] * factor


def body(n, nband, basis, hamiltonian, neighbours):
    bands, layers, cells, funcs = basis.shape
    total = layers * cells
    depth = layers * n
    rows = bands * nband // n
    n1 = 4
    n2 = n // n1
    first = lax.axis_index("elem") * layers
    layer_of = neighbours // cells
    cell_of = neighbours % cells
    inside = (layer_of - first) % depth * cells + cell_of
    low = jnp.concatenate([inside[0, :, :4], inside[0, :, 5:6], cell_of[0, :, 4:5]], axis=1)
    high = jnp.concatenate([inside[1, :, :4], inside[1, :, 4:5], cell_of[1, :, 5:6]], axis=1)
    tab = jnp.concatenate([low, high], axis=0).reshape(-1)
    y0 = basis.reshape(bands, total, funcs).transpose(1, 2, 0)
    ham = hamiltonian.reshape(total * 7, funcs, funcs)
    factor = 1.0 / (depth * cells * funcs)
    geom = (n, nband, cells, n1, n2, rows, factor)
    vm = pl.BlockSpec(memory_space=pltpu.VMEM)
    half = (cells, funcs, bands)
    dma = pltpu.SemaphoreType.DMA
    small = jax.ShapeDtypeStruct((rows, bands), F32)
    ft, s, p = pl.pallas_call(
        functools.partial(kernel, geom),
        out_shape=(jax.ShapeDtypeStruct((total, bands, funcs), BF16), small, small),
        in_specs=[
            pl.BlockSpec(memory_space=pltpu.SMEM),
            vm,
            pl.BlockSpec(memory_space=pl.ANY),
        ],
        out_specs=(vm, vm, vm),
        scratch_shapes=[
            pltpu.VMEM((total * 7, funcs, funcs), BF16),
            pltpu.VMEM((total, funcs, bands), BF16),
            pltpu.VMEM((total, funcs, bands), BF16),
            pltpu.VMEM(half, BF16),
            pltpu.VMEM(half, BF16),
            pltpu.VMEM(half, BF16),
            pltpu.VMEM(half, BF16),
            pltpu.VMEM((total, funcs, bands), F32),
            pltpu.VMEM((total, bands, funcs), BF16),
            pltpu.VMEM((nband - 1, total, funcs, bands), BF16),
            pltpu.VMEM((n1, n2, 2, rows, bands), F32),
            pltpu.VMEM((n1 - 1, n2, 2, rows, bands), F32),
            pltpu.VMEM((n2, 2, rows, bands), F32),
            pltpu.VMEM((n2 - 1, 2, rows, bands), F32),
            dma((4,)),
            dma((DEGREE + 1, 2)),
            dma((DEGREE + 1, 2)),
            dma((nband - 1, 2)),
            dma((nband - 1, 2)),
            dma((n1 - 1,)),
            dma((n1 - 1,)),
            dma((n2 - 1,)),
            dma((n2 - 1,)),
        ],
        compiler_params=pltpu.CompilerParams(
            collective_id=0, has_side_effects=True, vmem_limit_bytes=56 * 1024 * 1024
        ),
    )(tab, y0, ham)
    filtered = ft.transpose(1, 0, 2).reshape(bands, layers, cells, funcs)
    return filtered, s, p


def solution(mesh):
    placed = (
        P("band", "elem", None, None),
        P("elem", None, None, None, None),
        P("elem", None, None),
    )
    return jax.shard_map(
        functools.partial(body, mesh.shape["elem"], mesh.shape["band"]),
        mesh=mesh,
        in_specs=placed,
        out_specs=(P("band", "elem", None, None), P("elem", "band"), P("elem", "band")),
        check_vma=False,
    )
```

```python
import functools

import jax
import jax.numpy as jnp
from jax import lax
from jax.experimental import pallas as pl
from jax.experimental.pallas import tpu as pltpu
from jax.sharding import PartitionSpec as P

DEGREE = 4
FAR = 2
LATE = 2
MESH = pl.DeviceIdType.MESH
F32 = jnp.float32
BF16 = jnp.bfloat16


def dot(a, b):
    return jnp.dot(a, b, preferred_element_type=F32)


def kernel(
    geom,
    nbr,
    y0,
    ham_hbm,
    f_out,
    s_out,
    p_out,
    ham,
    buf_a,
    buf_b,
    near0,
    near1,
    far0,
    far1,
    acc,
    ft,
    it,
    others,
    parts,
    got1,
    mid,
    got2,
    ham_sem,
    out_sem,
    near_send,
    near_recv,
    far_send,
    far_recv,
    fsend,
    frecv,
    r1send,
    r1recv,
    r2send,
    r2recv,
):
    n, nband, cells, n1, n2, rows, factor = geom
    total = 2 * cells
    funcs, bands = y0.shape[1], y0.shape[2]
    me = lax.axis_index("elem")
    bme = lax.axis_index("band")
    right, left = lax.rem(me + 1, n), lax.rem(me + n - 1, n)
    group, member = me // n1, me % n1

    hcopies = []
    hparts = ham_sem.shape[0]
    for c in range(hparts):
        size = ham.shape[0] // hparts
        window = pl.ds(c * size, size)
        hc = pltpu.make_async_copy(ham_hbm.at[window], ham.at[window], ham_sem.at[c])
        hc.start()
        hcopies.append(hc)

    barrier = pltpu.get_barrier_semaphore()
    peers = [{"elem": left}, {"elem": right}]
    for j in range(1, nband):
        peers.append({"band": lax.rem(bme + j, nband)})
    for j in range(1, n1):
        peers.append({"elem": group * n1 + lax.rem(member + j, n1)})
    for j in range(1, n2):
        peers.append({"elem": lax.rem(group + j, n2) * n1 + member})
    for peer in peers:
        pl.semaphore_signal(barrier, inc=1, device_id=peer, device_id_type=MESH)
    pl.semaphore_wait(barrier, len(peers))

    core = me % 2
    near_base, far_base = (1 - core) * cells, core * cells
    near_face, far_face = 6 - core, 5 + core
    near_peer = me + 1 - 2 * core
    far_peer = lax.rem(me + n - 1 + 2 * core, n)
    nears, fars = (near0, near1), (far0, far1)
    piece = cells // FAR

    def near_copy(step, source):
        return pltpu.make_async_remote_copy(
            src_ref=source.at[pl.ds(near_base, cells)],
            dst_ref=nears[step % 2],
            send_sem=near_send.at[step],
            recv_sem=near_recv.at[step],
            device_id={"elem": near_peer},
            device_id_type=MESH,
        )

    def far_copy(step, source, c):
        return pltpu.make_async_remote_copy(
            src_ref=source.at[pl.ds(far_base + c * piece, piece)],
            dst_ref=fars[step % 2].at[pl.ds(c * piece, piece)],
            send_sem=far_send.at[step, c],
            recv_sem=far_recv.at[step, c],
            device_id={"elem": far_peer},
            device_id_type=MESH,
        )

    fcopies = []

    def send_field(layer, base):
        window = pl.ds(base, cells)
        for j in range(1, nband):
            copy = pltpu.make_async_remote_copy(
                src_ref=buf_a.at[window],
                dst_ref=others.at[j - 1, layer],
                send_sem=fsend.at[j - 1, layer],
                recv_sem=frecv.at[j - 1, layer],
                device_id={"band": lax.rem(bme + j, nband)},
                device_id_type=MESH,
            )
            copy.start()
            fcopies.append((j, layer, copy))

    late = (member == 0) | (member == n1 - 1)
    near = near_copy(0, y0)
    far = [far_copy(0, y0, c) for c in range(FAR)]

    @pl.when(jnp.logical_not(late))
    def _():
        for copy in far:
            copy.start()

    near.start()
    for c, hc in enumerate(hcopies):
        hc.wait()
        if c == LATE:

            @pl.when(late)
            def _():
                for copy in far:
                    copy.start()

    current = y0
    for step in range(DEGREE + 1):
        last = step == DEGREE
        target = buf_b if step % 2 == 0 else buf_a
        prior = y0 if step == 1 else target

        def local(e, carry, current=current):
            layer, cell = e // cells, e % cells
            base, own = e * 7, layer * cells
            total_ = dot(ham[base], current[e])
            for d in range(4):
                total_ += dot(
                    ham[base + d + 1], current[own + lax.rem(nbr[d, layer, cell], cells)]
                )
            there = cells - own + lax.rem(nbr[5 - layer, layer, cell], cells)
            total_ += dot(ham[base + 6 - layer], current[there])
            acc[e] = total_
            return carry

        lax.fori_loop(0, total, local, 0)

        def finish(i, carry, halo, base, face, step=step, target=target, prior=prior):
            e = base + i
            index = lax.rem(nbr[face - 1, base // cells, i], cells)
            value = acc[e] + dot(ham[e * 7 + face], halo[index])
            if step > 0 and step < DEGREE:
                value = 2.0 * value - prior[e].astype(F32)
            if step < DEGREE:
                target[e] = value.astype(BF16)
            else:
                it[e] = value.T.astype(BF16)
            return carry

        near.wait_recv()
        at_near = functools.partial(
            finish, halo=nears[step % 2], base=near_base, face=near_face
        )
        at_far = functools.partial(
            finish, halo=fars[step % 2], base=far_base, face=far_face
        )
        near_next, far_next = None, []
        lax.fori_loop(0, cells, at_near, 0)
        if not last:
            near_next = near_copy(step + 1, target)
            near_next.start()
        if step == DEGREE - 1:
            send_field(0, near_base)
        for copy in far:
            copy.wait_recv()
        if last:
            lax.fori_loop(0, cells, at_far, 0)
        else:
            for c in range(FAR):
                lax.fori_loop(c * piece, (c + 1) * piece, at_far, 0)
                copy = far_copy(step + 1, target, c)
                copy.start()
                far_next.append(copy)
        if step == DEGREE - 1:
            send_field(1, far_base)
            written = pltpu.make_async_copy(buf_a, f_out, out_sem)
            written.start()

            def turn(e, carry):
                ft[e] = buf_a[e].astype(F32).T.astype(BF16)
                return carry

            lax.fori_loop(0, total, turn, 0)
        near.wait_send()
        for copy in far:
            copy.wait_send()
        near, far = near_next, far_next
        current = target

    per = bands // rows

    def gram(field, first, count, state):
        def body(i, carry):
            s, p = carry
            v = field(i)
            e = first + i
            return s + dot(ft[e], v), p + dot(it[e], v)

        return lax.fori_loop(0, count, body, state)

    def put(who, state):
        for t in range(2):
            block = state[t].T.reshape(per, rows, bands)
            for i in range(per):
                r = who * per + i
                parts[r % n1, r // n1, t] = block[i]

    zero = jnp.zeros((bands, bands), F32)
    put(bme, gram(lambda e: buf_a[e], 0, total, (zero, zero)))
    for j in range(1, nband):
        state = (zero, zero)
        for jj, layer, copy in fcopies:
            if jj == j:
                copy.wait_recv()
                base = near_base if layer == 0 else far_base
                state = gram(lambda i: others[j - 1, layer, i], base, cells, state)
        put(lax.rem(bme + nband - j, nband), state)

    copies = []
    for j in range(1, n1):
        to = lax.rem(member + j, n1)
        copy = pltpu.make_async_remote_copy(
            src_ref=parts.at[to],
            dst_ref=got1.at[j - 1],
            send_sem=r1send.at[j - 1],
            recv_sem=r1recv.at[j - 1],
            device_id={"elem": group * n1 + to},
            device_id_type=MESH,
        )
        copy.start()
        copies.append(copy)
    for _, _, copy in fcopies:
        copy.wait_send()
    running = parts[member]
    for j, copy in enumerate(copies):
        copy.wait_recv()
        running += got1[j]
    mid[...] = running
    copies2 = []
    for j in range(1, n2):
        to = lax.rem(group + j, n2)
        copy = pltpu.make_async_remote_copy(
            src_ref=mid.at[to],
            dst_ref=got2.at[j - 1],
            send_sem=r2send.at[j - 1],
            recv_sem=r2recv.at[j - 1],
            device_id={"elem": to * n1 + member},
            device_id_type=MESH,
        )
        copy.start()
        copies2.append(copy)
    for copy in copies:
        copy.wait_send()
    final = mid[group]
    for j, copy in enumerate(copies2):
        copy.wait_recv()
        final += got2[j]
    for copy in copies2:
        copy.wait_send()
    written.wait()
    s_out[...] = final[0] * factor
    p_out[...] = final[1] * factor


def body(n, nband, basis, hamiltonian, neighbours):
    bands, layers, cells, funcs = basis.shape
    total = layers * cells
    depth = layers * n
    rows = bands * nband // n
    n1 = 4
    n2 = n // n1
    nbr = neighbours.transpose(2, 0, 1)
    y0 = basis.reshape(bands, total, funcs).transpose(1, 2, 0)
    ham = hamiltonian.reshape(total * 7, funcs, funcs)
    factor = 1.0 / (depth * cells * funcs)
    geom = (n, nband, cells, n1, n2, rows, factor)
    vm = pl.BlockSpec(memory_space=pltpu.VMEM)
    half = (cells, funcs, bands)
    dma = pltpu.SemaphoreType.DMA
    small = jax.ShapeDtypeStruct((rows, bands), F32)
    field, s, p = pl.pallas_call(
        functools.partial(kernel, geom),
        out_shape=(jax.ShapeDtypeStruct((total, funcs, bands), BF16), small, small),
        in_specs=[
            pl.BlockSpec(memory_space=pltpu.SMEM),
            vm,
            pl.BlockSpec(memory_space=pl.ANY),
        ],
        out_specs=(pl.BlockSpec(memory_space=pl.ANY), vm, vm),
        scratch_shapes=[
            pltpu.VMEM((total * 7, funcs, funcs), BF16),
            pltpu.VMEM((total, funcs, bands), BF16),
            pltpu.VMEM((total, funcs, bands), BF16),
            pltpu.VMEM(half, BF16),
            pltpu.VMEM(half, BF16),
            pltpu.VMEM(half, BF16),
            pltpu.VMEM(half, BF16),
            pltpu.VMEM((total, funcs, bands), F32),
            pltpu.VMEM((total, bands, funcs), BF16),
            pltpu.VMEM((total, bands, funcs), BF16),
            pltpu.VMEM((nband - 1, 2, cells, funcs, bands), BF16),
            pltpu.VMEM((n1, n2, 2, rows, bands), F32),
            pltpu.VMEM((n1 - 1, n2, 2, rows, bands), F32),
            pltpu.VMEM((n2, 2, rows, bands), F32),
            pltpu.VMEM((n2 - 1, 2, rows, bands), F32),
            dma((4,)),
            dma,
            dma((DEGREE + 1,)),
            dma((DEGREE + 1,)),
            dma((DEGREE + 1, FAR)),
            dma((DEGREE + 1, FAR)),
            dma((nband - 1, 2)),
            dma((nband - 1, 2)),
            dma((n1 - 1,)),
            dma((n1 - 1,)),
            dma((n2 - 1,)),
            dma((n2 - 1,)),
        ],
        compiler_params=pltpu.CompilerParams(
            collective_id=0, has_side_effects=True, vmem_limit_bytes=56 * 1024 * 1024
        ),
    )(nbr, y0, ham)
    filtered = field.transpose(2, 0, 1).reshape(bands, layers, cells, funcs)
    return filtered, s, p


def solution(mesh):
    placed = (
        P("band", "elem", None, None),
        P("elem", None, None, None, None),
        P("elem", None, None),
    )
    return jax.shard_map(
        functools.partial(body, mesh.shape["elem"], mesh.shape["band"]),
        mesh=mesh,
        in_specs=placed,
        out_specs=(P("band", "elem", None, None), P("elem", "band"), P("elem", "band")),
        check_vma=False,
    )
```

```python
import functools

import jax
import jax.numpy as jnp
from jax import lax
from jax.experimental import pallas as pl
from jax.experimental.pallas import tpu as pltpu
from jax.sharding import PartitionSpec as P

DEGREE = 4
FAR = 2
LATE = 2
MESH = pl.DeviceIdType.MESH
F32 = jnp.float32
BF16 = jnp.bfloat16


def dot(a, b):
    return jnp.dot(a, b, preferred_element_type=F32)


def kernel(
    geom,
    nbr,
    y0,
    ham_hbm,
    f_out,
    s_out,
    p_out,
    ham,
    buf_a,
    buf_b,
    near0,
    near1,
    far0,
    far1,
    acc,
    ft,
    it,
    others,
    parts,
    got1,
    mid,
    got2,
    ham_sem,
    out_sem,
    near_send,
    near_recv,
    far_send,
    far_recv,
    fsend,
    frecv,
    r1send,
    r1recv,
    r2send,
    r2recv,
):
    n, nband, cells, n1, n2, rows, factor = geom
    total = 2 * cells
    funcs, bands = y0.shape[1], y0.shape[2]
    me = lax.axis_index("elem")
    bme = lax.axis_index("band")
    right, left = lax.rem(me + 1, n), lax.rem(me + n - 1, n)
    group, member = me // n1, me % n1

    hcopies = []
    hparts = ham_sem.shape[0]
    for c in range(hparts):
        size = ham.shape[0] // hparts
        window = pl.ds(c * size, size)
        hc = pltpu.make_async_copy(ham_hbm.at[window], ham.at[window], ham_sem.at[c])
        hc.start()
        hcopies.append(hc)

    barrier = pltpu.get_barrier_semaphore()
    peers = [{"elem": left}, {"elem": right}]
    for j in range(1, nband):
        peers.append({"band": lax.rem(bme + j, nband)})
    for j in range(1, n1):
        peers.append({"elem": group * n1 + lax.rem(member + j, n1)})
    for j in range(1, n2):
        peers.append({"elem": lax.rem(group + j, n2) * n1 + member})
    for peer in peers:
        pl.semaphore_signal(barrier, inc=1, device_id=peer, device_id_type=MESH)
    pl.semaphore_wait(barrier, len(peers))

    core = me % 2
    near_base, far_base = (1 - core) * cells, core * cells
    near_face, far_face = 6 - core, 5 + core
    near_peer = me + 1 - 2 * core
    far_peer = lax.rem(me + n - 1 + 2 * core, n)
    nears, fars = (near0, near1), (far0, far1)
    piece = cells // FAR

    def near_copy(step, source):
        return pltpu.make_async_remote_copy(
            src_ref=source.at[pl.ds(near_base, cells)],
            dst_ref=nears[step % 2],
            send_sem=near_send.at[step],
            recv_sem=near_recv.at[step],
            device_id={"elem": near_peer},
            device_id_type=MESH,
        )

    def far_copy(step, source, c):
        return pltpu.make_async_remote_copy(
            src_ref=source.at[pl.ds(far_base + c * piece, piece)],
            dst_ref=fars[step % 2].at[pl.ds(c * piece, piece)],
            send_sem=far_send.at[step, c],
            recv_sem=far_recv.at[step, c],
            device_id={"elem": far_peer},
            device_id_type=MESH,
        )

    fcopies = []

    def send_field(layer, base):
        window = pl.ds(base, cells)
        for j in range(1, nband):
            copy = pltpu.make_async_remote_copy(
                src_ref=buf_a.at[window],
                dst_ref=others.at[j - 1, layer],
                send_sem=fsend.at[j - 1, layer],
                recv_sem=frecv.at[j - 1, layer],
                device_id={"band": lax.rem(bme + j, nband)},
                device_id_type=MESH,
            )
            copy.start()
            fcopies.append((j, layer, copy))

    late = (member == 0) | (member == n1 - 1)
    near = near_copy(0, y0)
    far = [far_copy(0, y0, c) for c in range(FAR)]

    @pl.when(jnp.logical_not(late))
    def _():
        for copy in far:
            copy.start()

    near.start()
    for c, hc in enumerate(hcopies):
        hc.wait()
        if c == LATE:

            @pl.when(late)
            def _():
                for copy in far:
                    copy.start()

    current = y0
    for step in range(DEGREE + 1):
        last = step == DEGREE
        target = buf_b if step % 2 == 0 else buf_a
        prior = y0 if step == 1 else target

        def local(e, carry, current=current):
            layer, cell = e // cells, e % cells
            base, own = e * 7, layer * cells
            total_ = dot(ham[base], current[e])
            for d in range(4):
                total_ += dot(
                    ham[base + d + 1], current[own + lax.rem(nbr[d, layer, cell], cells)]
                )
            there = cells - own + lax.rem(nbr[5 - layer, layer, cell], cells)
            total_ += dot(ham[base + 6 - layer], current[there])
            acc[e] = total_
            return carry

        lax.fori_loop(0, total, local, 0, unroll=4)

        def finish(i, carry, halo, base, face, step=step, target=target, prior=prior):
            e = base + i
            index = lax.rem(nbr[face - 1, base // cells, i], cells)
            value = acc[e] + dot(ham[e * 7 + face], halo[index])
            if step > 0 and step < DEGREE:
                value = 2.0 * value - prior[e].astype(F32)
            if step < DEGREE:
                target[e] = value.astype(BF16)
            else:
                it[e] = value.T.astype(BF16)
            return carry

        near.wait_recv()
        at_near = functools.partial(
            finish, halo=nears[step % 2], base=near_base, face=near_face
        )
        at_far = functools.partial(
            finish, halo=fars[step % 2], base=far_base, face=far_face
        )
        near_next, far_next = None, []
        lax.fori_loop(0, cells, at_near, 0, unroll=4)
        if not last:
            near_next = near_copy(step + 1, target)
            near_next.start()
        if step == DEGREE - 1:
            send_field(0, near_base)
        for copy in far:
            copy.wait_recv()
        if last:
            lax.fori_loop(0, cells, at_far, 0, unroll=4)
        else:
            for c in range(FAR):
                lax.fori_loop(c * piece, (c + 1) * piece, at_far, 0, unroll=4)
                copy = far_copy(step + 1, target, c)
                copy.start()
                far_next.append(copy)
        if step == DEGREE - 1:
            send_field(1, far_base)
            written = pltpu.make_async_copy(buf_a, f_out, out_sem)
            written.start()

            def turn(e, carry):
                ft[e] = buf_a[e].astype(F32).T.astype(BF16)
                return carry

            lax.fori_loop(0, total, turn, 0, unroll=4)
        near.wait_send()
        for copy in far:
            copy.wait_send()
        near, far = near_next, far_next
        current = target

    per = bands // rows

    def gram(field, first, count, state):
        def body(i, carry):
            s, p = carry
            v = field(i)
            e = first + i
            return s + dot(ft[e], v), p + dot(it[e], v)

        return lax.fori_loop(0, count, body, state, unroll=4)

    def put(who, state):
        for t in range(2):
            block = state[t].T.reshape(per, rows, bands)
            for i in range(per):
                r = who * per + i
                parts[r % n1, r // n1, t] = block[i]

    zero = jnp.zeros((bands, bands), F32)
    put(bme, gram(lambda e: buf_a[e], 0, total, (zero, zero)))
    for j in range(1, nband):
        state = (zero, zero)
        for jj, layer, copy in fcopies:
            if jj == j:
                copy.wait_recv()
                base = near_base if layer == 0 else far_base
                state = gram(lambda i: others[j - 1, layer, i], base, cells, state)
        put(lax.rem(bme + nband - j, nband), state)

    copies = []
    for j in range(1, n1):
        to = lax.rem(member + j, n1)
        copy = pltpu.make_async_remote_copy(
            src_ref=parts.at[to],
            dst_ref=got1.at[j - 1],
            send_sem=r1send.at[j - 1],
            recv_sem=r1recv.at[j - 1],
            device_id={"elem": group * n1 + to},
            device_id_type=MESH,
        )
        copy.start()
        copies.append(copy)
    for _, _, copy in fcopies:
        copy.wait_send()
    running = parts[member]
    for j, copy in enumerate(copies):
        copy.wait_recv()
        running += got1[j]
    mid[...] = running
    copies2 = []
    for j in range(1, n2):
        to = lax.rem(group + j, n2)
        copy = pltpu.make_async_remote_copy(
            src_ref=mid.at[to],
            dst_ref=got2.at[j - 1],
            send_sem=r2send.at[j - 1],
            recv_sem=r2recv.at[j - 1],
            device_id={"elem": to * n1 + member},
            device_id_type=MESH,
        )
        copy.start()
        copies2.append(copy)
    for copy in copies:
        copy.wait_send()
    final = mid[group]
    for j, copy in enumerate(copies2):
        copy.wait_recv()
        final += got2[j]
    for copy in copies2:
        copy.wait_send()
    written.wait()
    s_out[...] = final[0] * factor
    p_out[...] = final[1] * factor


def body(n, nband, basis, hamiltonian, neighbours):
    bands, layers, cells, funcs = basis.shape
    total = layers * cells
    depth = layers * n
    rows = bands * nband // n
    n1 = 4
    n2 = n // n1
    nbr = neighbours.transpose(2, 0, 1)
    y0 = basis.reshape(bands, total, funcs).transpose(1, 2, 0)
    ham = hamiltonian.reshape(total * 7, funcs, funcs)
    factor = 1.0 / (depth * cells * funcs)
    geom = (n, nband, cells, n1, n2, rows, factor)
    vm = pl.BlockSpec(memory_space=pltpu.VMEM)
    half = (cells, funcs, bands)
    dma = pltpu.SemaphoreType.DMA
    small = jax.ShapeDtypeStruct((rows, bands), F32)
    field, s, p = pl.pallas_call(
        functools.partial(kernel, geom),
        out_shape=(jax.ShapeDtypeStruct((total, funcs, bands), BF16), small, small),
        in_specs=[
            pl.BlockSpec(memory_space=pltpu.SMEM),
            vm,
            pl.BlockSpec(memory_space=pl.ANY),
        ],
        out_specs=(pl.BlockSpec(memory_space=pl.ANY), vm, vm),
        scratch_shapes=[
            pltpu.VMEM((total * 7, funcs, funcs), BF16),
            pltpu.VMEM((total, funcs, bands), BF16),
            pltpu.VMEM((total, funcs, bands), BF16),
            pltpu.VMEM(half, BF16),
            pltpu.VMEM(half, BF16),
            pltpu.VMEM(half, BF16),
            pltpu.VMEM(half, BF16),
            pltpu.VMEM((total, funcs, bands), F32),
            pltpu.VMEM((total, bands, funcs), BF16),
            pltpu.VMEM((total, bands, funcs), BF16),
            pltpu.VMEM((nband - 1, 2, cells, funcs, bands), BF16),
            pltpu.VMEM((n1, n2, 2, rows, bands), F32),
            pltpu.VMEM((n1 - 1, n2, 2, rows, bands), F32),
            pltpu.VMEM((n2, 2, rows, bands), F32),
            pltpu.VMEM((n2 - 1, 2, rows, bands), F32),
            dma((4,)),
            dma,
            dma((DEGREE + 1,)),
            dma((DEGREE + 1,)),
            dma((DEGREE + 1, FAR)),
            dma((DEGREE + 1, FAR)),
            dma((nband - 1, 2)),
            dma((nband - 1, 2)),
            dma((n1 - 1,)),
            dma((n1 - 1,)),
            dma((n2 - 1,)),
            dma((n2 - 1,)),
        ],
        compiler_params=pltpu.CompilerParams(
            collective_id=0, has_side_effects=True, vmem_limit_bytes=56 * 1024 * 1024
        ),
    )(nbr, y0, ham)
    filtered = field.transpose(2, 0, 1).reshape(bands, layers, cells, funcs)
    return filtered, s, p


def solution(mesh):
    placed = (
        P("band", "elem", None, None),
        P("elem", None, None, None, None),
        P("elem", None, None),
    )
    return jax.shard_map(
        functools.partial(body, mesh.shape["elem"], mesh.shape["band"]),
        mesh=mesh,
        in_specs=placed,
        out_specs=(P("band", "elem", None, None), P("elem", "band"), P("elem", "band")),
        check_vma=False,
    )
```
